512 devices in a mesh: ctx: 128 (over z, y, core), head: 4 (over x).
Axes of the slice: x: 4, y: 8, z: 8, core: 2. Of those that a mesh axis runs over, the one named last changes fastest.
Arguments:
- query_rows: bfloat16 [65536, 1536], P(('ctx', 'head')), may hold values from -51 to 51
- key_rows: bfloat16 [65536, 1536], P(('ctx', 'head')), may hold values from -6 to 6
- value_rows: bfloat16 [65536, 1536], P(('ctx', 'head')), may hold values from -12 to 12
- residual: bfloat16 [65536, 1536], P(('ctx', 'head')), may hold values from -6 to 6
- levels: int32 [128], P('ctx'), may hold values from 0 to 49
- gate_table: float32 [50, 1536], replicated, may hold values from -4 to 4
- block_mask: int32 [128, 7, 4, 4], P('ctx'), may hold values from 0 to 1, as said below
- out_weight: bfloat16 [1536, 1536], P('head'), may hold values from -0.15625 to 0.15625
Outputs:
- mixed: bfloat16 [65536, 1536], P(('ctx', 'head'))
The draws below stay inside these ranges and needn't reach their ends.
Inputs may be any that keep to these rules, and one draw needn't show every extreme that they name: block_mask[f, s, a, b] = 1 lets query block a of frame f attend key block b of frame f + offset(s); slot 0 is all ones; entries whose frame f + offset(s) lies outside the clip are 0.
All inputs are finite; a program needn't handle non-finite values.
Results may differ from the reference program's by a relative error of at most 0.0065.
Values may be sent and summed in bfloat16 or wider, within the bound.
No kernel may reach another device: no remote copies, remote signals or barrier semaphores. Data moves between devices by JAX's collectives and lax.ppermute only.
A program may use at most 64 MiB of HBM per device.

```python
import math
import jax
import jax.numpy as jnp
from jax import lax

D = 1536
HEADS = 12
HEAD_DIM = 128
FRAME = 512
BLOCK = 128
LOGR = 3
LEVELS = 50
SLOTS = 7
FRAMES = 128
TOKENS = 65536
BLOCKS = 4


def drawn_pair(key):
    key_first = jax.random.fold_in(key, 11)
    key_second = jax.random.fold_in(key, 23)
    keys_base = jnp.clip(jax.random.normal(key_first, (TOKENS, D), jnp.float32), -6.0, 6.0)
    queries = jnp.clip(1.5 * jax.random.normal(key_second, (TOKENS, D), jnp.float32), -9.0, 9.0)
    return (queries, keys_base)


def draw_query_rows(key, part):
    return drawn_pair(key)[0].astype(jnp.bfloat16)


def draw_key_rows(key, part):
    return drawn_pair(key)[1].astype(jnp.bfloat16)


def draw_block_mask(key, part):
    dice_rolls = jax.random.randint(key, (FRAMES, SLOTS, BLOCKS, BLOCKS), 0, 2 ** LOGR, dtype=jnp.int32)
    slot_ids = jnp.arange(SLOTS, dtype=jnp.int32)
    octave = jnp.maximum((slot_ids - 1) // 2, 0)
    distance = jnp.left_shift(jnp.ones_like(octave), octave)
    offset_row = jnp.where(slot_ids == 0, 0, jnp.where(slot_ids % 2 == 1, -distance, distance))
    partner = jnp.arange(FRAMES, dtype=jnp.int32)[:, None] + offset_row[None, :]
    inside = (partner >= 0) & (partner < FRAMES)
    threshold = jnp.left_shift(jnp.ones_like(octave), LOGR - 1 - octave)
    kept_pairs = (dice_rolls < threshold[None, :, None, None]) & inside[:, :, None, None]
    kept_pairs = kept_pairs | (slot_ids == 0)[None, :, None, None]
    return kept_pairs.astype(jnp.int32)


def place_ends(result, stream_key, low, largest):
    extent = result.shape
    index_at = [jax.random.randint(jax.random.fold_in(stream_key, axis), (), 0, extent[axis]) for axis in range(len(extent))]
    result = result.at[tuple(index_at)].set(low)
    longest = extent.index(max(extent))
    index_at[longest] = (index_at[longest] + 1) % extent[longest]
    return result.at[tuple(index_at)].set(largest)


def steps_of(own_key, shape, pieces, smallest, largest):
    def one(dim, shards_of):
        steps = jax.random.uniform(jax.random.fold_in(jax.random.fold_in(own_key, 6), dim), (shards_of,), jnp.float32, smallest / len(pieces), largest / len(pieces))
        return jnp.repeat(jnp.exp(steps), shape[dim] // shards_of).reshape((-1,) + (1,) * (len(shape) - dim - 1))

    loudness = one(*pieces[0])
    for cut in pieces[1:]:
        loudness = loudness * one(*cut)
    return loudness


def bell_draw(stream_key, shape, width, most, split=(), held_as=jnp.bfloat16):
    array = jax.random.normal(stream_key, shape, jnp.float32) * width
    if len(split) > 0:
        array = steps_of(stream_key, shape, split, -0.22, 0.18) * array
    return jnp.clip(array, min=-most, max=most).astype(held_as)


def setup_inputs(seed: int = 0) -> dict:
    arg_keys = jax.random.split(jax.random.key(seed), 9)
    return {
        "query_rows": draw_query_rows(jax.random.fold_in(arg_keys[8], 71), 0),
        "key_rows": draw_key_rows(jax.random.fold_in(arg_keys[8], 71), 0),
        "value_rows": bell_draw(arg_keys[2], (TOKENS, D), 2.0, 12.0, ((0, 512),)),
        "residual": bell_draw(arg_keys[3], (TOKENS, D), 1.0, 6.0, ((0, 512),)),
        "levels": place_ends(jax.random.randint(arg_keys[4], (FRAMES,), 0, LEVELS), jax.random.fold_in(arg_keys[4], 1), 0, LEVELS - 1).astype(jnp.int32),
        "gate_table": bell_draw(arg_keys[5], (LEVELS, D), 1.0, 4.0, (), jnp.float32),
        "block_mask": draw_block_mask(jax.random.fold_in(arg_keys[8], 71), 0),
        "out_weight": bell_draw(arg_keys[7], (D, D), D ** -0.5, 0.15625, ((0, 4),)),
    }


def offset_list():
    found_offsets = [0]
    for octave in range(LOGR):
        found_offsets.append(-2 ** octave)
        found_offsets.append(2 ** octave)
    return found_offsets

def expand_blocks(block_rows):
    blocks = block_rows.shape[0]
    broadened = jnp.broadcast_to(block_rows[:, None, :, None], (blocks, BLOCK, blocks, BLOCK))
    return broadened.reshape(blocks * BLOCK, blocks * BLOCK) > 0

def reference(query_rows, key_rows, value_rows, residual, levels, gate_table, block_mask, out_weight):
    queries_all = query_rows.reshape(FRAMES, FRAME, HEADS, HEAD_DIM)
    keys_all = key_rows.reshape(FRAMES, FRAME, HEADS, HEAD_DIM)
    values_all = value_rows.reshape(FRAMES, FRAME, HEADS, HEAD_DIM)
    inv_root = 1.0 / math.sqrt(HEAD_DIM)

    def one_frame(frame_idx):
        query_block = queries_all[frame_idx].astype(jnp.float32)
        score_list = []
        value_list = []
        for slot_idx, shift_by in enumerate(offset_list()):
            partner = jnp.clip(frame_idx + shift_by, 0, FRAMES - 1).astype(jnp.int32)
            key_block = keys_all[partner].astype(jnp.float32)
            value_block = values_all[partner].astype(jnp.float32)
            allowed = expand_blocks(block_mask[frame_idx, slot_idx])
            scores = jnp.einsum('qhd,khd->hqk', query_block, key_block) * inv_root
            score_list.append(jnp.where(allowed[None], scores, -jnp.inf))
            value_list.append(value_block)
        scores = jnp.concatenate(score_list, axis=2)
        values = jnp.concatenate(value_list, axis=0)
        row_max = lax.optimization_barrier(jnp.max(scores, axis=2, keepdims=True))
        exp_scores = jnp.exp(scores - row_max)
        row_total = lax.optimization_barrier(jnp.sum(exp_scores, axis=2))
        weights = lax.optimization_barrier(exp_scores.astype(jnp.bfloat16)).astype(jnp.float32)
        summed = jnp.einsum('hqk,khd->qhd', weights, values)
        return (summed / jnp.transpose(row_total)[:, :, None]).astype(jnp.bfloat16)
    attention = lax.map(one_frame, jnp.arange(FRAMES, dtype=jnp.int32))
    attention = attention.reshape(TOKENS, D)
    projected = jnp.dot(attention, out_weight, preferred_element_type=jnp.float32)
    gate_rows = jnp.repeat(gate_table[levels], FRAME, axis=0)
    return (residual.astype(jnp.float32) + gate_rows * projected).astype(jnp.bfloat16)
```

```python
import math

import jax
import jax.numpy as jnp
from jax import lax
from jax.experimental import pallas as pl
from jax.experimental.pallas import tpu as pltpu
from jax.sharding import PartitionSpec as P


HEAD_DIM = 128
BLOCK = 128
EXP2_SCALE = math.log2(math.e) / math.sqrt(HEAD_DIM)
SMEM = pl.BlockSpec(memory_space=pltpu.SMEM)
VMEM = pl.BlockSpec(memory_space=pltpu.VMEM)


def to_frame(x, source_of):
    count = lax.axis_size("ctx")
    pairs = [(source_of(f), f) for f in range(count) if 0 <= source_of(f) < count]
    return lax.ppermute(x, "ctx", pairs)


def partner(f):
    return f ^ 1


def outward(f):
    return f + 2 if f % 2 == 0 else f - 2


def inward(f):
    return f - 2 if f % 2 == 0 else f + 2


def along_head(x, by):
    size = lax.axis_size("head")
    return lax.ppermute(x, "head", [(i, (i + by) % size) for i in range(size)])


def exchange(pieces):
    return lax.all_to_all(pieces, "head", 0, 0, tiled=True)


def pack_kernel(*refs):
    row_refs, out_ref = refs[:-1], refs[-1]
    for i, rows in enumerate(row_refs):
        for h in range(out_ref.shape[2]):
            out_ref[0, i, h] = rows[:, h * HEAD_DIM : (h + 1) * HEAD_DIM]


def pack(arrays, groups):
    tokens, width = arrays[0].shape
    heads = width // HEAD_DIM // groups
    shape = (groups, len(arrays), heads, tokens, HEAD_DIM)
    return pl.pallas_call(
        pack_kernel,
        grid=(groups,),
        in_specs=[pl.BlockSpec((tokens, width // groups), lambda g: (0, g))] * len(arrays),
        out_specs=pl.BlockSpec((1, *shape[1:]), lambda g: (g, 0, 0, 0, 0)),
        out_shape=jax.ShapeDtypeStruct(shape, arrays[0].dtype),
        name="pack",
    )(*arrays)


def deal_kernel(place_ref, rows_ref, *out_refs):
    groups, heads = len(out_refs), out_refs[0].shape[0]
    for r, out_ref in enumerate(out_refs):
        group = (place_ref[1] + r) % groups
        for h in range(heads):
            at = pl.multiple_of((group * heads + h) * HEAD_DIM, HEAD_DIM)
            out_ref[h] = rows_ref[:, pl.ds(at, HEAD_DIM)]


def deal(place, rows, groups):
    tokens, width = rows.shape
    shape = (width // HEAD_DIM // groups, tokens, HEAD_DIM)
    return pl.pallas_call(
        deal_kernel,
        in_specs=[SMEM, VMEM],
        out_specs=[VMEM] * groups,
        out_shape=[jax.ShapeDtypeStruct(shape, rows.dtype)] * groups,
        name="deal",
    )(place, rows)


def attend_kernel(slots, groups, first, last, place_ref, mask_ref, *refs):
    count = len(slots)
    q_refs, kv_refs, refs = refs[:groups], refs[groups : groups + count], refs[groups + count :]
    rows = groups * BLOCK
    core, x = place_ref[0], place_ref[1]
    queries = jnp.concatenate([q[0] for q in q_refs], axis=0)
    if first:
        outs = refs
    else:
        acc_in, stat_in = refs[:2]
        outs = refs[2:]
    scores = [
        lax.dot_general(
            queries,
            kv[:, 0, 0].reshape(rows, HEAD_DIM),
            (((1,), (1,)), ((), ())),
            preferred_element_type=jnp.float32,
        )
        for kv in kv_refs
    ]
    slot_at = [jnp.where(core == 0, even, odd) * groups * groups for even, odd in slots]
    weights, maxima, totals, rescales = [], [], [], []
    for r in range(groups):
        own = slice(r * BLOCK, (r + 1) * BLOCK)
        q_block = (x + groups - r) % groups
        tiles = []
        for s in range(count):
            for b in range(groups):
                keep = mask_ref[slot_at[s] + q_block * groups + b] > 0
                tile = scores[s][own, b * BLOCK : (b + 1) * BLOCK]
                tiles.append(jnp.where(keep, tile, -jnp.inf))
        peak = tiles[0]
        for tile in tiles[1:]:
            peak = jnp.maximum(peak, tile)
        peak = jnp.max(peak, axis=1, keepdims=True)
        if not first:
            before = stat_in[0, own, 0:1]
            peak = jnp.maximum(peak, before)
            rescale = jnp.exp2((before - peak) * EXP2_SCALE)
        tiles = [jnp.exp2((tile - peak) * EXP2_SCALE) for tile in tiles]
        total = tiles[0]
        for tile in tiles[1:]:
            total = total + tile
        total = jnp.sum(total, axis=1, keepdims=True)
        if not first:
            total = total + stat_in[0, own, 1:2] * rescale
            rescales.append(rescale)
        maxima.append(peak)
        totals.append(total)
        weights.append(jnp.concatenate([t.astype(jnp.bfloat16) for t in tiles], axis=1))
    weights = jnp.concatenate(weights, axis=0)
    values = jnp.concatenate([kv[:, 1, 0].reshape(rows, HEAD_DIM) for kv in kv_refs], axis=0)
    weighted = jnp.dot(weights, values, preferred_element_type=jnp.float32)
    total = jnp.concatenate(totals, axis=0)
    if not first:
        weighted = weighted + acc_in[0] * jnp.concatenate(rescales, axis=0)
    if last:
        attention = (weighted / total).astype(jnp.bfloat16)
        for r in range(groups):
            outs[0][(x + groups - r) % groups, 0] = attention[r * BLOCK : (r + 1) * BLOCK]
    else:
        acc_out, stat_out = outs
        acc_out[0] = weighted
        lane = lax.broadcasted_iota(jnp.int32, (rows, HEAD_DIM), 1)
        stat_out[0] = jnp.where(lane == 0, jnp.concatenate(maxima, axis=0), total)


def attend(slots, place, mask, queries, kvs, state, last):
    groups, (heads, tokens, _) = len(queries), queries[0].shape
    rows = groups * tokens
    q_spec = pl.BlockSpec((1, tokens, HEAD_DIM), lambda h: (h, 0, 0))
    kv_spec = pl.BlockSpec((groups, 2, 1, tokens, HEAD_DIM), lambda h: (0, 0, h, 0, 0))
    state_spec = pl.BlockSpec((1, rows, HEAD_DIM), lambda h: (h, 0, 0))
    state_shape = jax.ShapeDtypeStruct((heads, rows, HEAD_DIM), jnp.float32)
    extra = () if state is None else state
    if last:
        out_shape = jax.ShapeDtypeStruct((groups, heads, tokens, HEAD_DIM), jnp.bfloat16)
        out_specs = pl.BlockSpec((groups, 1, tokens, HEAD_DIM), lambda h: (0, h, 0, 0))
    else:
        out_shape, out_specs = (state_shape, state_shape), (state_spec, state_spec)

    def kernel(*refs):
        attend_kernel(slots, groups, state is None, last, *refs)

    return pl.pallas_call(
        kernel,
        grid=(heads,),
        in_specs=[SMEM, SMEM]
        + [q_spec] * groups
        + [kv_spec] * len(kvs)
        + [state_spec] * len(extra),
        out_specs=out_specs,
        out_shape=out_shape,
    )(place, mask, *queries, *kvs, *extra)


def project_kernel(place_ref, o_ref, w_ref, m1, m2, m3, other_ref, gate_ref, residual_ref, out_ref):
    groups, heads = o_ref.shape[0], o_ref.shape[1]
    core, x = place_ref[0], place_ref[1]
    half = m1.shape[1]
    features = []
    for r in range(groups):
        group = (x + groups - r) % groups
        features.append(jnp.concatenate([o_ref[group, h] for h in range(heads)], axis=1))
    mine = [m1[...], m2[...], m3[...]]
    other = [other_ref[i] for i in range(groups - 1)]
    for column, far in ((core, mine), (1 - core, other)):
        at = pl.ds(pl.multiple_of(column * half, 128), half)
        projected = jnp.dot(features[0], w_ref[:, at], preferred_element_type=jnp.float32)
        for rows, weight in zip(features[1:], far, strict=True):
            projected += jnp.dot(rows, weight, preferred_element_type=jnp.float32)
        mixed = residual_ref[:, at].astype(jnp.float32) + gate_ref[:, at] * projected
        out_ref[:, at] = mixed.astype(jnp.bfloat16)


def project(place, gathered, weight, mine, other, gate, residual):
    return pl.pallas_call(
        project_kernel,
        in_specs=[SMEM] + [VMEM] * 8,
        out_specs=VMEM,
        out_shape=jax.ShapeDtypeStruct(residual.shape, jnp.bfloat16),
        name="project",
    )(place, gathered, weight, *mine, other, gate, residual)


def after(value, *others):
    return lax.optimization_barrier((value, *others))[0]


def body(query_rows, key_rows, value_rows, residual, levels, gate_table, block_mask, out_weight):
    groups = lax.axis_size("head")
    core = lax.axis_index("ctx") % 2
    place = jnp.stack([core, lax.axis_index("head")])
    mask = block_mask.reshape(-1)
    half = out_weight.shape[1] // 2

    kv_send = pack((key_rows, value_rows), groups)
    own = exchange(kv_send)
    dealt = deal(place, after(query_rows, kv_send), groups)
    queries = [dealt[0], None, None, None]
    for r in (1, 3, 2):
        queries[r] = along_head(dealt[r], r)
    gate = lax.dynamic_slice_in_dim(gate_table, levels[0], 1, axis=0)
    weight_half = after(lax.dynamic_slice_in_dim(out_weight, core * half, half, axis=1), kv_send)
    mine = [None, None, None]
    for r in (1, 3, 2):
        mine[r - 1] = along_head(weight_half, r)

    first = to_frame(own, outward)
    swapped = to_frame(own, partner)
    second = to_frame(own, inward)
    far_first = to_frame(first, outward)
    swapped_first = to_frame(first, partner)
    far_second = to_frame(second, inward)

    state = attend(((0, 0), (2, 1)), place, mask, queries, [own, swapped], None, False)
    state = attend(
        ((4, 3), (1, 2), (3, 4)),
        place,
        mask,
        queries,
        [first, swapped_first, second],
        state,
        False,
    )
    other = to_frame(jnp.stack([after(m, state[0]) for m in mine]), partner)
    state = attend(((6, 5),), place, mask, queries, [far_first], state, False)
    attention = attend(((5, 6),), place, mask, queries, [far_second], state, True)
    gathered = exchange(attention)
    return project(place, gathered, out_weight, mine, other, gate, residual)


def solution(mesh):
    return jax.shard_map(
        body,
        mesh=mesh,
        in_specs=(
            P(("ctx", "head"), None),
            P(("ctx", "head"), None),
            P(("ctx", "head"), None),
            P(("ctx", "head"), None),
            P("ctx"),
            P(),
            P("ctx", None, None, None),
            P("head", None),
        ),
        out_specs=P(("ctx", "head"), None),
        check_vma=False,
    )
```

```python
import math

import jax
import jax.numpy as jnp
from jax import lax
from jax.experimental import pallas as pl
from jax.experimental.pallas import tpu as pltpu
from jax.sharding import PartitionSpec as P


HEAD_DIM = 128
BLOCK = 128
EXP2_SCALE = math.log2(math.e) / math.sqrt(HEAD_DIM)
SMEM = pl.BlockSpec(memory_space=pltpu.SMEM)
VMEM = pl.BlockSpec(memory_space=pltpu.VMEM)


def to_frame(x, source_of):
    count = lax.axis_size("ctx")
    pairs = [(source_of(f), f) for f in range(count) if 0 <= source_of(f) < count]
    return lax.ppermute(x, "ctx", pairs)


def partner(f):
    return f ^ 1


def outward(f):
    return f + 2 if f % 2 == 0 else f - 2


def inward(f):
    return f - 2 if f % 2 == 0 else f + 2


def beside(x):
    frames, size = lax.axis_size("ctx"), lax.axis_size("head")
    pairs = [
        (f * size + (i + 1 - 2 * (f % 2)) % size, f * size + i)
        for f in range(frames)
        for i in range(size)
    ]
    return lax.ppermute(x, ("ctx", "head"), pairs)


def exchange(pieces):
    return lax.all_to_all(pieces, "head", 0, 0, tiled=True)


def call(kernel, args, out_shape):
    specs = [SMEM if a.dtype == jnp.int32 else VMEM for a in args]
    args = [
        a if a.dtype == jnp.int32 else pltpu.with_memory_space_constraint(a, pltpu.VMEM)
        for a in args
    ]
    return pl.pallas_call(
        kernel,
        in_specs=specs,
        out_specs=jax.tree.map(lambda _: VMEM, out_shape),
        out_shape=out_shape,
        compiler_params=pltpu.CompilerParams(vmem_limit_bytes=24 << 20),
    )(*args)


def pack_kv_kernel(key_ref, value_ref, out_ref):
    groups, _, heads = out_ref.shape[:3]
    for g in range(groups):
        for h in range(heads):
            at = slice((g * heads + h) * HEAD_DIM, (g * heads + h + 1) * HEAD_DIM)
            out_ref[g, 0, h] = key_ref[:, at]
            out_ref[g, 1, h] = jnp.transpose(value_ref[:, at])


def pack_q_kernel(query_ref, out_ref):
    groups, heads = out_ref.shape[:2]
    for g in range(groups):
        for h in range(heads):
            out_ref[g, h] = query_ref[:, (g * heads + h) * HEAD_DIM : (g * heads + h + 1) * HEAD_DIM]


def attend_kernel(slots, first, last, place_ref, mask_ref, q_ref, *refs):
    count = len(slots)
    kv_refs, refs = refs[:count], refs[count:]
    groups, heads = q_ref.shape[:2]
    rows = groups * BLOCK
    core = place_ref[0]
    if first:
        outs = refs
    else:
        peak_in, total_in, acc_in = refs[:3]
        outs = refs[3:]
    slot_at = [jnp.where(core == 0, even, odd) * groups * groups for even, odd in slots]
    keep = [
        [[mask_ref[slot_at[s] + a * groups + b] > 0 for a in range(groups)] for b in range(groups)]
        for s in range(count)
    ]
    for h in range(heads):
        queries = q_ref[:, h].reshape(rows, HEAD_DIM)
        tiles, peak = [], None
        for s in range(count):
            for b in range(groups):
                tile = lax.dot_general(
                    kv_refs[s][b, 0, h],
                    queries,
                    (((1,), (1,)), ((), ())),
                    preferred_element_type=jnp.float32,
                )
                tile = jnp.concatenate(
                    [
                        jnp.where(keep[s][b][a], tile[:, a * BLOCK : (a + 1) * BLOCK], -jnp.inf)
                        for a in range(groups)
                    ],
                    axis=1,
                )
                top = jnp.max(tile.reshape(BLOCK // 8, 8, rows), axis=0)
                peak = top if peak is None else jnp.maximum(peak, top)
                tiles.append(tile)
        peak = jnp.max(peak, axis=0, keepdims=True)
        if not first:
            before = peak_in[h, 0:1]
            peak = jnp.maximum(peak, before)
            rescale = jnp.exp2((before - peak) * EXP2_SCALE)
        total, weights = None, []
        for tile in tiles:
            tile = jnp.exp2((tile - peak) * EXP2_SCALE)
            part = jnp.sum(tile.reshape(BLOCK // 8, 8, rows), axis=0)
            total = part if total is None else total + part
            weights.append(tile.astype(jnp.bfloat16))
        values = jnp.concatenate(
            [kv_refs[s][b, 1, h] for s in range(count) for b in range(groups)], axis=1
        )
        weighted = jnp.dot(
            values, jnp.concatenate(weights, axis=0), preferred_element_type=jnp.float32
        )
        if not first:
            total = total + total_in[h] * rescale
            weighted = weighted + acc_in[h] * rescale
        if last:
            total = jnp.sum(total, axis=0, keepdims=True)
            attention = (weighted / total).astype(jnp.bfloat16)
            for a in range(groups):
                outs[0][a, h] = jnp.transpose(attention[:, a * BLOCK : (a + 1) * BLOCK])
        else:
            outs[0][h] = jnp.broadcast_to(peak, (8, rows))
            outs[1][h] = total
            outs[2][h] = weighted


def attend(slots, place, mask, queries, kvs, state, last):
    groups, heads, tokens = queries.shape[:3]
    rows = groups * tokens
    if last:
        out_shape = jax.ShapeDtypeStruct(queries.shape, jnp.bfloat16)
    else:
        stat = jax.ShapeDtypeStruct((heads, 8, rows), jnp.float32)
        out_shape = [stat, stat, jax.ShapeDtypeStruct((heads, HEAD_DIM, rows), jnp.float32)]

    def kernel(*refs):
        attend_kernel(slots, state is None, last, *refs)

    return call(kernel, (place, mask, queries, *kvs, *(state or ())), out_shape)


def project_kernel(
    place_ref, o_ref, own_ref, near_ref, far_ref, mine_ref, other_ref, gate_ref, residual_ref, out_ref
):
    groups, heads = o_ref.shape[:2]
    core, x = place_ref[0], place_ref[1]
    half = mine_ref.shape[1]

    def features(up):
        group = (x + up) % groups
        return jnp.concatenate([o_ref[group, h] for h in range(heads)], axis=1)

    step = 1 + 2 * core
    own, near, far, opposite = features(0), features(step), features(4 - step), features(2)
    for column, opposite_ref in ((core, mine_ref), (1 - core, other_ref)):
        at = pl.ds(pl.multiple_of(column * half, 128), half)
        projected = jnp.dot(own, own_ref[:, at], preferred_element_type=jnp.float32)
        projected += jnp.dot(near, near_ref[:, at], preferred_element_type=jnp.float32)
        projected += jnp.dot(far, far_ref[:, at], preferred_element_type=jnp.float32)
        projected += jnp.dot(opposite, opposite_ref[...], preferred_element_type=jnp.float32)
        mixed = residual_ref[:, at].astype(jnp.float32) + gate_ref[:, at] * projected
        out_ref[:, at] = mixed.astype(jnp.bfloat16)


def after(value, *others):
    return lax.optimization_barrier((value, *others))[0]


def body(query_rows, key_rows, value_rows, residual, levels, gate_table, block_mask, out_weight):
    groups = lax.axis_size("head")
    tokens, width = query_rows.shape
    heads = width // HEAD_DIM // groups
    core = lax.axis_index("ctx") % 2
    place = jnp.stack([core, lax.axis_index("head")])
    mask = block_mask.reshape(-1)
    half = width // 2

    kv_shape = jax.ShapeDtypeStruct((groups, 2, heads, tokens, HEAD_DIM), jnp.bfloat16)
    q_shape = jax.ShapeDtypeStruct((groups, heads, tokens, HEAD_DIM), jnp.bfloat16)
    kv_send = call(pack_kv_kernel, (key_rows, value_rows), kv_shape)
    own = exchange(kv_send)
    q_send = call(pack_q_kernel, (after(query_rows, kv_send),), q_shape)
    gate = lax.dynamic_slice_in_dim(gate_table, levels[0], 1, axis=0)
    near = beside(after(out_weight, kv_send))

    first = to_frame(own, outward)
    second = to_frame(own, inward)
    queries = exchange(after(q_send, own))
    swapped = to_frame(own, partner)
    mine = beside(lax.dynamic_slice_in_dim(near, core * half, half, axis=1))
    far_first = to_frame(first, outward)
    far_second = to_frame(second, inward)
    swapped_first = to_frame(first, partner)
    far = to_frame(near, partner)
    other = to_frame(mine, partner)

    state = attend(((0, 0), (2, 1)), place, mask, queries, [own, swapped], None, False)
    slots = ((4, 3), (1, 2), (3, 4))
    arrived = [first, swapped_first, second]
    state = attend(slots, place, mask, queries, arrived, state, False)
    state = attend(((6, 5),), place, mask, queries, [far_first], state, False)
    attention = attend(((5, 6),), place, mask, queries, [far_second], state, True)
    gathered = exchange(attention)
    return call(
        project_kernel,
        (place, gathered, out_weight, near, far, mine, other, gate, residual),
        jax.ShapeDtypeStruct(residual.shape, jnp.bfloat16),
    )


def solution(mesh):
    return jax.shard_map(
        body,
        mesh=mesh,
        in_specs=(
            P(("ctx", "head"), None),
            P(("ctx", "head"), None),
            P(("ctx", "head"), None),
            P(("ctx", "head"), None),
            P("ctx"),
            P(),
            P("ctx", None, None, None),
            P("head", None),
        ),
        out_specs=P(("ctx", "head"), None),
        check_vma=False,
    )
```

```python
import math

import jax
import jax.numpy as jnp
from jax import lax
from jax.experimental import pallas as pl
from jax.experimental.pallas import tpu as pltpu
from jax.sharding import PartitionSpec as P


HEAD_DIM = 128
BLOCK = 128
EXP2_SCALE = math.log2(math.e) / math.sqrt(HEAD_DIM)
SMEM = pl.BlockSpec(memory_space=pltpu.SMEM)
VMEM = pl.BlockSpec(memory_space=pltpu.VMEM)


def to_frame(x, source_of):
    count = lax.axis_size("ctx")
    pairs = [(source_of(f), f) for f in range(count) if 0 <= source_of(f) < count]
    return lax.ppermute(x, "ctx", pairs)


def partner(f):
    return f ^ 1


def outward(f):
    return f + 2 if f % 2 == 0 else f - 2


def inward(f):
    return f - 2 if f % 2 == 0 else f + 2


def beside(x):
    frames, size = lax.axis_size("ctx"), lax.axis_size("head")
    pairs = [
        (f * size + (i + 1 - 2 * (f % 2)) % size, f * size + i)
        for f in range(frames)
        for i in range(size)
    ]
    return lax.ppermute(x, ("ctx", "head"), pairs)


def exchange(pieces):
    return lax.all_to_all(pieces, "head", 0, 0, tiled=True)


def call(kernel, args, out_shape):
    specs = [SMEM if a.dtype == jnp.int32 else VMEM for a in args]
    args = [
        a if a.dtype == jnp.int32 else pltpu.with_memory_space_constraint(a, pltpu.VMEM)
        for a in args
    ]
    return pl.pallas_call(
        kernel,
        in_specs=specs,
        out_specs=jax.tree.map(lambda _: VMEM, out_shape),
        out_shape=out_shape,
        compiler_params=pltpu.CompilerParams(vmem_limit_bytes=8 << 20),
    )(*args)


def pack_kv_kernel(key_hbm, value_hbm, out_ref, key_ref, value_ref, sems):
    groups, _, heads = out_ref.shape[:3]
    fetch_value = pltpu.make_async_copy(value_hbm, value_ref, sems.at[0])
    fetch_key = pltpu.make_async_copy(key_hbm, key_ref, sems.at[1])
    fetch_value.start()
    fetch_key.start()
    places = [(g, h) for g in range(groups) for h in range(heads)]
    fetch_value.wait()
    for g, h in places:
        at = slice((g * heads + h) * HEAD_DIM, (g * heads + h + 1) * HEAD_DIM)
        out_ref[g, 1, h] = jnp.transpose(value_ref[:, at])
    fetch_key.wait()
    for g, h in places:
        at = slice((g * heads + h) * HEAD_DIM, (g * heads + h + 1) * HEAD_DIM)
        out_ref[g, 0, h] = key_ref[:, at]


def pack_kv(key_rows, value_rows, shape):
    hbm = pl.BlockSpec(memory_space=pltpu.HBM)
    args = [pltpu.with_memory_space_constraint(a, pltpu.HBM) for a in (key_rows, value_rows)]
    return pl.pallas_call(
        pack_kv_kernel,
        in_specs=[hbm, hbm],
        out_specs=VMEM,
        out_shape=jax.ShapeDtypeStruct(shape, jnp.bfloat16),
        scratch_shapes=[pltpu.VMEM(a.shape, a.dtype) for a in args]
        + [pltpu.SemaphoreType.DMA((2,))],
        name="pack_kv",
        compiler_params=pltpu.CompilerParams(vmem_limit_bytes=8 << 20),
    )(*args)


def pack_q_kernel(query_ref, out_ref):
    groups, heads = out_ref.shape[:2]
    for g in range(groups):
        for h in range(heads):
            out_ref[g, h] = query_ref[:, (g * heads + h) * HEAD_DIM : (g * heads + h + 1) * HEAD_DIM]


def half_kernel(place_ref, weight_ref, out_ref):
    width = out_ref.shape[1]
    out_ref[...] = weight_ref[:, pl.ds(pl.multiple_of(place_ref[0] * width, 128), width)]


def attend_kernel(slots, first, last, place_ref, mask_ref, q_ref, *refs):
    count = len(slots)
    kv_refs, refs = refs[:count], refs[count:]
    groups, heads = q_ref.shape[:2]
    rows = groups * BLOCK
    core = place_ref[0]
    if first:
        outs = refs
    else:
        peak_in, total_in, acc_in = refs[:3]
        outs = refs[3:]
    slot_at = [jnp.where(core == 0, even, odd) * groups * groups for even, odd in slots]
    keep = [
        [[mask_ref[slot_at[s] + a * groups + b] > 0 for a in range(groups)] for b in range(groups)]
        for s in range(count)
    ]
    ones = jnp.ones((16, count * rows), jnp.bfloat16)

    def score(h):
        keys = jnp.concatenate([kv[:, 0, h].reshape(rows, HEAD_DIM) for kv in kv_refs], axis=0)
        return lax.dot_general(
            keys,
            q_ref[:, h].reshape(rows, HEAD_DIM),
            (((1,), (1,)), ((), ())),
            preferred_element_type=jnp.float32,
        )

    def soften(h, scores):
        tiles, peak = [], None
        for i in range(count * groups):
            tile = jnp.concatenate(
                [
                    jnp.where(
                        keep[i // groups][i % groups][a],
                        scores[i * BLOCK : (i + 1) * BLOCK, a * BLOCK : (a + 1) * BLOCK],
                        -jnp.inf,
                    )
                    for a in range(groups)
                ],
                axis=1,
            )
            top = jnp.max(tile.reshape(BLOCK // 8, 8, rows), axis=0)
            peak = top if peak is None else jnp.maximum(peak, top)
            tiles.append(tile)
        peak = jnp.max(peak, axis=0, keepdims=True)
        if not first:
            peak = jnp.maximum(peak, peak_in[h, 0:1])
        weights = [jnp.exp2((tile - peak) * EXP2_SCALE).astype(jnp.bfloat16) for tile in tiles]
        return peak, jnp.concatenate(weights, axis=0)

    def gather(h, peak, weights):
        values = jnp.concatenate(
            [kv[b, 1, h] for kv in kv_refs for b in range(groups)], axis=1
        )
        weighted = jnp.dot(
            jnp.concatenate([values, ones], axis=0), weights, preferred_element_type=jnp.float32
        )
        total, weighted = weighted[HEAD_DIM : HEAD_DIM + 8], weighted[:HEAD_DIM]
        if not first:
            rescale = jnp.exp2((peak_in[h, 0:1] - peak) * EXP2_SCALE)
            total = total + total_in[h] * rescale
            weighted = weighted + acc_in[h] * rescale
        if last:
            attention = (weighted / total[0:1]).astype(jnp.bfloat16)
            for a in range(groups):
                outs[0][a, h] = jnp.transpose(attention[:, a * BLOCK : (a + 1) * BLOCK])
        else:
            outs[0][h] = jnp.broadcast_to(peak, (8, rows))
            outs[1][h] = total
            outs[2][h] = weighted

    scores = score(0)
    for h in range(heads):
        ahead = score(h + 1) if h + 1 < heads else None
        gather(h, *soften(h, scores))
        scores = ahead


def attend(slots, place, mask, queries, kvs, state, last):
    groups, heads, tokens = queries.shape[:3]
    rows = groups * tokens
    if last:
        out_shape = jax.ShapeDtypeStruct(queries.shape, jnp.bfloat16)
    else:
        stat = jax.ShapeDtypeStruct((heads, 8, rows), jnp.float32)
        out_shape = [stat, stat, jax.ShapeDtypeStruct((heads, HEAD_DIM, rows), jnp.float32)]

    def kernel(*refs):
        attend_kernel(slots, state is None, last, *refs)

    return call(kernel, (place, mask, queries, *kvs, *(state or ())), out_shape)


def project_kernel(
    place_ref, level_ref, o_ref, near_ref, mine_ref, other_ref, own_hbm, far_hbm, gate_hbm,
    residual_hbm, out_ref, own_ref, far_ref, gate_ref, residual_ref, sems,
):
    pairs = (
        (own_hbm, own_ref), (far_hbm, far_ref), (gate_hbm, gate_ref), (residual_hbm, residual_ref)
    )
    copies = [pltpu.make_async_copy(*pair, sems.at[i]) for i, pair in enumerate(pairs)]
    for copy in copies:
        copy.start()
    groups, heads = o_ref.shape[:2]
    core, x = place_ref[0], place_ref[1]
    half = mine_ref.shape[1]

    def features(up):
        group = (x + up) % groups
        return jnp.concatenate([o_ref[group, h] for h in range(heads)], axis=1)

    step = 1 + 2 * core
    own, near, far, opposite = features(0), features(step), features(4 - step), features(2)
    ats = [pl.ds(pl.multiple_of(c * half, 128), half) for c in (core, 1 - core)]
    sums = [
        jnp.dot(near, near_ref[:, at], preferred_element_type=jnp.float32)
        + jnp.dot(opposite, opposite_ref[...], preferred_element_type=jnp.float32)
        for at, opposite_ref in zip(ats, (mine_ref, other_ref), strict=True)
    ]
    for copy, rows, weight_ref in zip(copies, (own, far), (own_ref, far_ref)):
        copy.wait()
        sums = [
            total + jnp.dot(rows, weight_ref[:, at], preferred_element_type=jnp.float32)
            for at, total in zip(ats, sums, strict=True)
        ]
    for copy in copies[2:]:
        copy.wait()
    for at, total in zip(ats, sums, strict=True):
        gate = gate_ref[pl.ds(level_ref[0], 1), at]
        mixed = residual_ref[:, at].astype(jnp.float32) + gate * total
        out_ref[:, at] = mixed.astype(jnp.bfloat16)


def project(scalars, resident, fetched):
    hbm = pl.BlockSpec(memory_space=pltpu.HBM)
    residual = fetched[-1]
    return pl.pallas_call(
        project_kernel,
        in_specs=[SMEM] * len(scalars) + [VMEM] * len(resident) + [hbm] * len(fetched),
        out_specs=VMEM,
        out_shape=jax.ShapeDtypeStruct(residual.shape, residual.dtype),
        scratch_shapes=[pltpu.VMEM(a.shape, a.dtype) for a in fetched]
        + [pltpu.SemaphoreType.DMA((len(fetched),))],
        name="project",
        compiler_params=pltpu.CompilerParams(vmem_limit_bytes=16 << 20),
    )(
        *scalars,
        *(pltpu.with_memory_space_constraint(a, pltpu.VMEM) for a in resident),
        *(pltpu.with_memory_space_constraint(a, pltpu.HBM) for a in fetched),
    )


def after(value, *others):
    return lax.optimization_barrier((value, *others))[0]


def body(query_rows, key_rows, value_rows, residual, levels, gate_table, block_mask, out_weight):
    groups = lax.axis_size("head")
    tokens, width = query_rows.shape
    heads = width // HEAD_DIM // groups
    core = lax.axis_index("ctx") % 2
    place = jnp.stack([core, lax.axis_index("head")])
    mask = block_mask.reshape(-1)

    q_shape = jax.ShapeDtypeStruct((groups, heads, tokens, HEAD_DIM), jnp.bfloat16)
    kv_send = pack_kv(key_rows, value_rows, (groups, 2, heads, tokens, HEAD_DIM))
    own = exchange(kv_send)
    q_send = call(pack_q_kernel, (after(query_rows, kv_send, place, mask),), q_shape)
    near = beside(after(out_weight, kv_send))

    first = to_frame(own, outward)
    second = to_frame(own, inward)
    queries = exchange(after(q_send, own))
    swapped = to_frame(own, partner)
    half_shape = jax.ShapeDtypeStruct((near.shape[0], width // 2), jnp.bfloat16)
    near_half = call(half_kernel, (place, near), half_shape)
    mine = beside(near_half)
    far_first = to_frame(first, outward)
    far_second = to_frame(second, inward)
    swapped_first = to_frame(first, partner)
    far = to_frame(near, partner)
    other = to_frame(mine, partner)

    state = attend(((0, 0), (2, 1)), place, mask, queries, [own, swapped], None, False)
    slots, arrived = ((4, 3), (1, 2), (3, 4)), [first, swapped_first, second]
    state = attend(slots, place, mask, queries, arrived, state, False)
    state = attend(((6, 5),), place, mask, queries, [far_first], state, False)
    attention = attend(((5, 6),), place, mask, queries, [far_second], state, True)
    gathered = exchange(attention)
    return project(
        (place, levels), (gathered, near, mine, other), (out_weight, far, gate_table, residual)
    )


def solution(mesh):
    return jax.shard_map(
        body,
        mesh=mesh,
        in_specs=(
            P(("ctx", "head"), None),
            P(("ctx", "head"), None),
            P(("ctx", "head"), None),
            P(("ctx", "head"), None),
            P("ctx"),
            P(),
            P("ctx", None, None, None),
            P("head", None),
        ),
        out_specs=P(("ctx", "head"), None),
        check_vma=False,
    )
```

```python
import math

import jax
import jax.numpy as jnp
from jax import lax
from jax.experimental import pallas as pl
from jax.experimental.pallas import tpu as pltpu
from jax.sharding import PartitionSpec as P


HEAD_DIM = 128
BLOCK = 128
EXP2_SCALE = math.log2(math.e) / math.sqrt(HEAD_DIM)
SMEM = pl.BlockSpec(memory_space=pltpu.SMEM)
VMEM = pl.BlockSpec(memory_space=pltpu.VMEM)


def to_frame(x, source_of):
    count = lax.axis_size("ctx")
    pairs = [(source_of(f), f) for f in range(count) if 0 <= source_of(f) < count]
    return lax.ppermute(x, "ctx", pairs)


def partner(f):
    return f ^ 1


def outward(f):
    return f + 2 if f % 2 == 0 else f - 2


def inward(f):
    return f - 2 if f % 2 == 0 else f + 2


def beside(x):
    frames, size = lax.axis_size("ctx"), lax.axis_size("head")
    pairs = [
        (f * size + (i + 1 - 2 * (f % 2)) % size, f * size + i)
        for f in range(frames)
        for i in range(size)
    ]
    return lax.ppermute(x, ("ctx", "head"), pairs)


def exchange(pieces):
    return lax.all_to_all(pieces, "head", 0, 0, tiled=True)


def call(kernel, args, out_shape):
    specs = [SMEM if a.dtype == jnp.int32 else VMEM for a in args]
    args = [
        a if a.dtype == jnp.int32 else pltpu.with_memory_space_constraint(a, pltpu.VMEM)
        for a in args
    ]
    return pl.pallas_call(
        kernel,
        in_specs=specs,
        out_specs=jax.tree.map(lambda _: VMEM, out_shape),
        out_shape=out_shape,
        compiler_params=pltpu.CompilerParams(vmem_limit_bytes=8 << 20),
    )(*args)


def pack_kv_kernel(key_hbm, value_hbm, out_ref, key_ref, value_ref, sems):
    groups, _, heads = out_ref.shape[:3]
    fetch_value = pltpu.make_async_copy(value_hbm, value_ref, sems.at[0])
    fetch_key = pltpu.make_async_copy(key_hbm, key_ref, sems.at[1])
    fetch_value.start()
    fetch_key.start()
    places = [(g, h) for g in range(groups) for h in range(heads)]
    fetch_value.wait()
    for g, h in places:
        at = slice((g * heads + h) * HEAD_DIM, (g * heads + h + 1) * HEAD_DIM)
        out_ref[g, 1, h] = jnp.transpose(value_ref[:, at])
    fetch_key.wait()
    for g, h in places:
        at = slice((g * heads + h) * HEAD_DIM, (g * heads + h + 1) * HEAD_DIM)
        out_ref[g, 0, h] = key_ref[:, at]


def pack_kv(key_rows, value_rows, shape):
    hbm = pl.BlockSpec(memory_space=pltpu.HBM)
    args = [pltpu.with_memory_space_constraint(a, pltpu.HBM) for a in (key_rows, value_rows)]
    return pl.pallas_call(
        pack_kv_kernel,
        in_specs=[hbm, hbm],
        out_specs=VMEM,
        out_shape=jax.ShapeDtypeStruct(shape, jnp.bfloat16),
        scratch_shapes=[pltpu.VMEM(a.shape, a.dtype) for a in args]
        + [pltpu.SemaphoreType.DMA((2,))],
        name="pack_kv",
        compiler_params=pltpu.CompilerParams(vmem_limit_bytes=8 << 20),
    )(*args)


def pack_q_kernel(query_ref, out_ref):
    groups, heads = out_ref.shape[:2]
    for g in range(groups):
        for h in range(heads):
            out_ref[g, h] = query_ref[:, (g * heads + h) * HEAD_DIM : (g * heads + h + 1) * HEAD_DIM]


def half_kernel(place_ref, weight_ref, out_ref):
    width = out_ref.shape[1]
    out_ref[...] = weight_ref[:, pl.ds(pl.multiple_of(place_ref[0] * width, 128), width)]


def attend_kernel(slots, first, last, place_ref, mask_ref, q_ref, *refs):
    count = len(slots)
    kv_refs, refs = refs[:count], refs[count:]
    groups, heads = q_ref.shape[:2]
    rows = groups * BLOCK
    core = place_ref[0]
    if first:
        outs = refs
    else:
        peak_in, total_in, acc_in = refs[:3]
        outs = refs[3:]
    slot_at = [jnp.where(core == 0, even, odd) * groups * groups for even, odd in slots]
    keep = [
        [[mask_ref[slot_at[s] + a * groups + b] > 0 for a in range(groups)] for b in range(groups)]
        for s in range(count)
    ]
    ones = jnp.ones((16, count * rows), jnp.bfloat16)

    def score(h):
        keys = jnp.concatenate([kv[:, 0, h].reshape(rows, HEAD_DIM) for kv in kv_refs], axis=0)
        return lax.dot_general(
            keys,
            q_ref[:, h].reshape(rows, HEAD_DIM),
            (((1,), (1,)), ((), ())),
            preferred_element_type=jnp.float32,
        )

    def soften(h, scores):
        tiles, peak = [], None
        for i in range(count * groups):
            tile = jnp.concatenate(
                [
                    jnp.where(
                        keep[i // groups][i % groups][a],
                        scores[i * BLOCK : (i + 1) * BLOCK, a * BLOCK : (a + 1) * BLOCK],
                        -jnp.inf,
                    )
                    for a in range(groups)
                ],
                axis=1,
            )
            top = jnp.max(tile.reshape(BLOCK // 8, 8, rows), axis=0)
            peak = top if peak is None else jnp.maximum(peak, top)
            tiles.append(tile)
        peak = jnp.max(peak, axis=0, keepdims=True)
        if not first:
            peak = jnp.maximum(peak, peak_in[h, 0:1])
        weights = [jnp.exp2((tile - peak) * EXP2_SCALE).astype(jnp.bfloat16) for tile in tiles]
        return peak, jnp.concatenate(weights, axis=0)

    def gather(h, peak, weights):
        values = jnp.concatenate(
            [kv[b, 1, h] for kv in kv_refs for b in range(groups)], axis=1
        )
        weighted = jnp.dot(
            jnp.concatenate([values, ones], axis=0), weights, preferred_element_type=jnp.float32
        )
        total, weighted = weighted[HEAD_DIM : HEAD_DIM + 8], weighted[:HEAD_DIM]
        if not first:
            rescale = jnp.exp2((peak_in[h, 0:1] - peak) * EXP2_SCALE)
            total = total + total_in[h] * rescale
            weighted = weighted + acc_in[h] * rescale
        if last:
            attention = (weighted / total[0:1]).astype(jnp.bfloat16)
            for a in range(groups):
                outs[0][a, h] = jnp.transpose(attention[:, a * BLOCK : (a + 1) * BLOCK])
        else:
            outs[0][h] = jnp.broadcast_to(peak, (8, rows))
            outs[1][h] = total
            outs[2][h] = weighted

    scores = score(0)
    for h in range(heads):
        ahead = score(h + 1) if h + 1 < heads else None
        gather(h, *soften(h, scores))
        scores = ahead


def attend(slots, place, mask, queries, kvs, state, last):
    groups, heads, tokens = queries.shape[:3]
    rows = groups * tokens
    if last:
        out_shape = jax.ShapeDtypeStruct(queries.shape, jnp.bfloat16)
    else:
        stat = jax.ShapeDtypeStruct((heads, 8, rows), jnp.float32)
        out_shape = [stat, stat, jax.ShapeDtypeStruct((heads, HEAD_DIM, rows), jnp.float32)]

    def kernel(*refs):
        attend_kernel(slots, state is None, last, *refs)

    return call(kernel, (place, mask, queries, *kvs, *(state or ())), out_shape)


def project_kernel(
    place_ref, level_ref, o_ref, near_ref, other_ref, mine_hbm, own_hbm, far_hbm, gate_hbm,
    residual_hbm, out_ref, mine_ref, own_ref, far_ref, gate_ref, residual_ref, sems,
):
    pairs = (
        (mine_hbm, mine_ref), (own_hbm, own_ref), (far_hbm, far_ref), (gate_hbm, gate_ref),
        (residual_hbm, residual_ref),
    )
    copies = [pltpu.make_async_copy(*pair, sems.at[i]) for i, pair in enumerate(pairs)]
    for copy in copies:
        copy.start()
    groups, heads = o_ref.shape[:2]
    core, x = place_ref[0], place_ref[1]
    half = mine_ref.shape[1]

    def features(up):
        group = (x + up) % groups
        return jnp.concatenate([o_ref[group, h] for h in range(heads)], axis=1)

    step = 1 + 2 * core
    own, near, far, opposite = features(0), features(step), features(4 - step), features(2)
    ats = [pl.ds(pl.multiple_of(c * half, 128), half) for c in (core, 1 - core)]
    sums = [jnp.dot(near, near_ref[:, at], preferred_element_type=jnp.float32) for at in ats]
    copies[0].wait()
    sums = [
        total + jnp.dot(opposite, opposite_ref[...], preferred_element_type=jnp.float32)
        for total, opposite_ref in zip(sums, (mine_ref, other_ref), strict=True)
    ]
    for copy, rows, weight_ref in zip(copies[1:], (own, far), (own_ref, far_ref)):
        copy.wait()
        sums = [
            total + jnp.dot(rows, weight_ref[:, at], preferred_element_type=jnp.float32)
            for at, total in zip(ats, sums, strict=True)
        ]
    for copy in copies[3:]:
        copy.wait()
    for at, total in zip(ats, sums, strict=True):
        gate = gate_ref[pl.ds(level_ref[0], 1), at]
        mixed = residual_ref[:, at].astype(jnp.float32) + gate * total
        out_ref[:, at] = mixed.astype(jnp.bfloat16)


def project(scalars, resident, fetched):
    hbm = pl.BlockSpec(memory_space=pltpu.HBM)
    residual = fetched[-1]
    return pl.pallas_call(
        project_kernel,
        in_specs=[SMEM] * len(scalars) + [VMEM] * len(resident) + [hbm] * len(fetched),
        out_specs=VMEM,
        out_shape=jax.ShapeDtypeStruct(residual.shape, residual.dtype),
        scratch_shapes=[pltpu.VMEM(a.shape, a.dtype) for a in fetched]
        + [pltpu.SemaphoreType.DMA((len(fetched),))],
        name="project",
        compiler_params=pltpu.CompilerParams(vmem_limit_bytes=16 << 20),
    )(
        *scalars,
        *(pltpu.with_memory_space_constraint(a, pltpu.VMEM) for a in resident),
        *(pltpu.with_memory_space_constraint(a, pltpu.HBM) for a in fetched),
    )


def after(value, *others):
    return lax.optimization_barrier((value, *others))[0]


def body(query_rows, key_rows, value_rows, residual, levels, gate_table, block_mask, out_weight):
    groups = lax.axis_size("head")
    tokens, width = query_rows.shape
    heads = width // HEAD_DIM // groups
    core = lax.axis_index("ctx") % 2
    place = jnp.stack([core, lax.axis_index("head")])
    mask = block_mask.reshape(-1)

    q_shape = jax.ShapeDtypeStruct((groups, heads, tokens, HEAD_DIM), jnp.bfloat16)
    kv_send = pack_kv(key_rows, value_rows, (groups, 2, heads, tokens, HEAD_DIM))
    own = exchange(kv_send)
    q_send = call(pack_q_kernel, (after(query_rows, kv_send, place, mask),), q_shape)
    near = beside(after(out_weight, kv_send))

    first = to_frame(own, outward)
    second = to_frame(own, inward)
    queries = exchange(after(q_send, own))
    swapped = to_frame(own, partner)
    half_shape = jax.ShapeDtypeStruct((near.shape[0], width // 2), jnp.bfloat16)
    near_half = call(half_kernel, (place, near), half_shape)
    mine = beside(near_half)
    far_first = to_frame(first, outward)
    far_second = to_frame(second, inward)
    swapped_first = to_frame(first, partner)
    far = to_frame(near, partner)
    other = to_frame(mine, partner)

    state = attend(((0, 0), (2, 1)), place, mask, queries, [own, swapped], None, False)
    slots, arrived = ((4, 3), (1, 2), (3, 4)), [first, swapped_first, second]
    state = attend(slots, place, mask, queries, arrived, state, False)
    state = attend(((6, 5),), place, mask, queries, [far_first], state, False)
    attention = attend(((5, 6),), place, mask, queries, [far_second], state, True)
    gathered = exchange(attention)
    return project(
        (place, levels), (gathered, near, other), (mine, out_weight, far, gate_table, residual)
    )


def solution(mesh):
    return jax.shard_map(
        body,
        mesh=mesh,
        in_specs=(
            P(("ctx", "head"), None),
            P(("ctx", "head"), None),
            P(("ctx", "head"), None),
            P(("ctx", "head"), None),
            P("ctx"),
            P(),
            P("ctx", None, None, None),
            P("head", None),
        ),
        out_specs=P(("ctx", "head"), None),
        check_vma=False,
    )
```

```python
import math

import jax
import jax.numpy as jnp
from jax import lax
from jax.experimental import pallas as pl
from jax.experimental.pallas import tpu as pltpu
from jax.sharding import PartitionSpec as P


HEAD_DIM = 128
BLOCK = 128
EXP2_SCALE = math.log2(math.e) / math.sqrt(HEAD_DIM)
SMEM = pl.BlockSpec(memory_space=pltpu.SMEM)
VMEM = pl.BlockSpec(memory_space=pltpu.VMEM)


def to_frame(x, source_of):
    count = lax.axis_size("ctx")
    pairs = [(source_of(f), f) for f in range(count) if 0 <= source_of(f) < count]
    return lax.ppermute(x, "ctx", pairs)


def partner(f):
    return f ^ 1


def outward(f):
    return f + 2 if f % 2 == 0 else f - 2


def inward(f):
    return f - 2 if f % 2 == 0 else f + 2


def beside(x):
    frames, size = lax.axis_size("ctx"), lax.axis_size("head")
    pairs = [
        (f * size + (i + 1 - 2 * (f % 2)) % size, f * size + i)
        for f in range(frames)
        for i in range(size)
    ]
    return lax.ppermute(x, ("ctx", "head"), pairs)


def exchange(pieces):
    return lax.all_to_all(pieces, "head", 0, 0, tiled=True)


def call(kernel, args, out_shape, out_specs=None, scratch_shapes=()):
    specs = [SMEM if a.dtype == jnp.int32 else VMEM for a in args]
    args = [
        a if a.dtype == jnp.int32 else pltpu.with_memory_space_constraint(a, pltpu.VMEM)
        for a in args
    ]
    return pl.pallas_call(
        kernel,
        in_specs=specs,
        out_specs=out_specs or jax.tree.map(lambda _: VMEM, out_shape),
        scratch_shapes=scratch_shapes,
        out_shape=out_shape,
        compiler_params=pltpu.CompilerParams(vmem_limit_bytes=8 << 20),
    )(*args)


def pack_kv_kernel(key_hbm, value_hbm, out_hbm, key_ref, value_ref, out_ref, sems):
    groups, _, heads = out_ref.shape[:3]
    width = heads * HEAD_DIM
    fetches = [
        [
            pltpu.make_async_copy(hbm.at[:, columns], ref.at[:, columns], sems.at[i, g])
            for i, (hbm, ref) in enumerate(((key_hbm, key_ref), (value_hbm, value_ref)))
        ]
        for g, columns in ((g, pl.ds(g * width, width)) for g in range(groups))
    ]
    sends = [
        pltpu.make_async_copy(out_ref.at[g], out_hbm.at[g], sems.at[2, g]) for g in range(groups)
    ]
    for pair in fetches:
        for fetch in pair:
            fetch.start()
    for g in range(groups):
        for fetch in fetches[g]:
            fetch.wait()
        for h in range(heads):
            at = slice((g * heads + h) * HEAD_DIM, (g * heads + h + 1) * HEAD_DIM)
            out_ref[g, 0, h] = key_ref[:, at]
            out_ref[g, 1, h] = jnp.transpose(value_ref[:, at])
        sends[g].start()
    for send in sends:
        send.wait()


def pack_kv(key_rows, value_rows, shape):
    hbm = pl.BlockSpec(memory_space=pltpu.HBM)
    args = [pltpu.with_memory_space_constraint(a, pltpu.HBM) for a in (key_rows, value_rows)]
    return pl.pallas_call(
        pack_kv_kernel,
        in_specs=[hbm, hbm],
        out_specs=hbm,
        out_shape=jax.ShapeDtypeStruct(shape, jnp.bfloat16),
        scratch_shapes=[pltpu.VMEM(a.shape, a.dtype) for a in args]
        + [pltpu.VMEM(shape, jnp.bfloat16), pltpu.SemaphoreType.DMA((3, shape[0]))],
        name="pack_kv",
        compiler_params=pltpu.CompilerParams(vmem_limit_bytes=8 << 20),
    )(*args)


def pack_q_kernel(query_ref, out_ref):
    groups, heads = out_ref.shape[:2]
    for g in range(groups):
        for h in range(heads):
            out_ref[g, h] = query_ref[:, (g * heads + h) * HEAD_DIM : (g * heads + h + 1) * HEAD_DIM]


def half_kernel(place_ref, weight_ref, out_ref):
    width = out_ref.shape[1]
    out_ref[...] = weight_ref[:, pl.ds(pl.multiple_of(place_ref[0] * width, 128), width)]


def attend_kernel(slots, first, last, place_ref, mask_ref, q_ref, *refs):
    count = len(slots)
    kv_refs, refs = refs[:count], refs[count:]
    groups, heads = q_ref.shape[:2]
    rows = groups * BLOCK
    core = place_ref[0]
    if first:
        outs = refs
    else:
        peak_in, total_in, acc_in = refs[:3]
        outs = refs[3:]
    slot_at = [jnp.where(core == 0, even, odd) * groups * groups for even, odd in slots]
    keep = [
        [[mask_ref[slot_at[s] + a * groups + b] > 0 for a in range(groups)] for b in range(groups)]
        for s in range(count)
    ]
    ones = jnp.ones((16, count * rows), jnp.bfloat16)

    def score(h):
        keys = jnp.concatenate([kv[:, 0, h].reshape(rows, HEAD_DIM) for kv in kv_refs], axis=0)
        return lax.dot_general(
            keys,
            q_ref[:, h].reshape(rows, HEAD_DIM),
            (((1,), (1,)), ((), ())),
            preferred_element_type=jnp.float32,
        )

    def soften(h, scores):
        tiles, peak = [], None
        for i in range(count * groups):
            tile = jnp.concatenate(
                [
                    jnp.where(
                        keep[i // groups][i % groups][a],
                        scores[i * BLOCK : (i + 1) * BLOCK, a * BLOCK : (a + 1) * BLOCK],
                        -jnp.inf,
                    )
                    for a in range(groups)
                ],
                axis=1,
            )
            top = jnp.max(tile.reshape(BLOCK // 8, 8, rows), axis=0)
            peak = top if peak is None else jnp.maximum(peak, top)
            tiles.append(tile)
        peak = jnp.max(peak, axis=0, keepdims=True)
        if not first:
            peak = jnp.maximum(peak, peak_in[h, 0:1])
        weights = [jnp.exp2((tile - peak) * EXP2_SCALE).astype(jnp.bfloat16) for tile in tiles]
        return peak, jnp.concatenate(weights, axis=0)

    def gather(h, peak, weights):
        values = jnp.concatenate(
            [kv[b, 1, h] for kv in kv_refs for b in range(groups)], axis=1
        )
        weighted = jnp.dot(
            jnp.concatenate([values, ones], axis=0), weights, preferred_element_type=jnp.float32
        )
        total, weighted = weighted[HEAD_DIM : HEAD_DIM + 8], weighted[:HEAD_DIM]
        if not first:
            rescale = jnp.exp2((peak_in[h, 0:1] - peak) * EXP2_SCALE)
            total = total + total_in[h] * rescale
            weighted = weighted + acc_in[h] * rescale
        if last:
            attention = (weighted / total[0:1]).astype(jnp.bfloat16)
            for a in range(groups):
                outs[1][a, h] = jnp.transpose(attention[:, a * BLOCK : (a + 1) * BLOCK])
            pltpu.make_async_copy(outs[1].at[:, h], outs[0].at[:, h], outs[2].at[h]).start()
        else:
            outs[0][h] = jnp.broadcast_to(peak, (8, rows))
            outs[1][h] = total
            outs[2][h] = weighted

    scores = score(0)
    for h in range(heads):
        ahead = score(h + 1) if h + 1 < heads else None
        gather(h, *soften(h, scores))
        scores = ahead
    if last:
        for h in range(heads):
            pltpu.make_async_copy(outs[1].at[:, h], outs[0].at[:, h], outs[2].at[h]).wait()


def attend(slots, place, mask, queries, kvs, state, last):
    groups, heads, tokens = queries.shape[:3]
    rows = groups * tokens
    out_specs, scratch_shapes = None, ()
    if last:
        out_shape = jax.ShapeDtypeStruct(queries.shape, jnp.bfloat16)
        out_specs = pl.BlockSpec(memory_space=pltpu.HBM)
        scratch_shapes = [
            pltpu.VMEM(queries.shape, jnp.bfloat16), pltpu.SemaphoreType.DMA((heads,))
        ]
    else:
        stat = jax.ShapeDtypeStruct((heads, 8, rows), jnp.float32)
        out_shape = [stat, stat, jax.ShapeDtypeStruct((heads, HEAD_DIM, rows), jnp.float32)]

    def kernel(*refs):
        attend_kernel(slots, state is None, last, *refs)

    args = (place, mask, queries, *kvs, *(state or ()))
    return call(kernel, args, out_shape, out_specs, scratch_shapes)


def project_kernel(
    place_ref, level_ref, o_ref, near_ref, far_ref, other_ref, mine_hbm, own_hbm, gate_hbm,
    residual_hbm, out_ref, mine_ref, own_ref, gate_ref, residual_ref, sems,
):
    pairs = (
        (mine_hbm, mine_ref), (own_hbm, own_ref), (gate_hbm, gate_ref),
        (residual_hbm, residual_ref),
    )
    copies = [pltpu.make_async_copy(*pair, sems.at[i]) for i, pair in enumerate(pairs)]
    for copy in copies:
        copy.start()
    groups, heads = o_ref.shape[:2]
    core, x = place_ref[0], place_ref[1]
    half = mine_ref.shape[1]

    def features(up):
        group = (x + up) % groups
        return jnp.concatenate([o_ref[group, h] for h in range(heads)], axis=1)

    step = 1 + 2 * core
    own, near, far, opposite = features(0), features(step), features(4 - step), features(2)
    ats = [pl.ds(pl.multiple_of(c * half, 128), half) for c in (core, 1 - core)]
    sums = [
        jnp.dot(near, near_ref[:, at], preferred_element_type=jnp.float32)
        + jnp.dot(far, far_ref[:, at], preferred_element_type=jnp.float32)
        for at in ats
    ]
    copies[0].wait()
    sums = [
        total + jnp.dot(opposite, opposite_ref[...], preferred_element_type=jnp.float32)
        for total, opposite_ref in zip(sums, (mine_ref, other_ref), strict=True)
    ]
    copies[1].wait()
    sums = [
        total + jnp.dot(own, own_ref[:, at], preferred_element_type=jnp.float32)
        for total, at in zip(sums, ats, strict=True)
    ]
    for copy in copies[2:]:
        copy.wait()
    for at, total in zip(ats, sums, strict=True):
        gate = gate_ref[pl.ds(level_ref[0], 1), at]
        mixed = residual_ref[:, at].astype(jnp.float32) + gate * total
        out_ref[:, at] = mixed.astype(jnp.bfloat16)


def project(scalars, resident, fetched):
    hbm = pl.BlockSpec(memory_space=pltpu.HBM)
    residual = fetched[-1]
    return pl.pallas_call(
        project_kernel,
        in_specs=[SMEM] * len(scalars) + [VMEM] * len(resident) + [hbm] * len(fetched),
        out_specs=VMEM,
        out_shape=jax.ShapeDtypeStruct(residual.shape, residual.dtype),
        scratch_shapes=[pltpu.VMEM(a.shape, a.dtype) for a in fetched]
        + [pltpu.SemaphoreType.DMA((len(fetched),))],
        name="project",
        compiler_params=pltpu.CompilerParams(vmem_limit_bytes=16 << 20),
    )(
        *scalars,
        *(pltpu.with_memory_space_constraint(a, pltpu.VMEM) for a in resident),
        *(pltpu.with_memory_space_constraint(a, pltpu.HBM) for a in fetched),
    )


def after(value, *others):
    return lax.optimization_barrier((value, *others))[0]


def body(query_rows, key_rows, value_rows, residual, levels, gate_table, block_mask, out_weight):
    groups = lax.axis_size("head")
    tokens, width = query_rows.shape
    heads = width // HEAD_DIM // groups
    core = lax.axis_index("ctx") % 2
    place = jnp.stack([core, lax.axis_index("head")])
    mask = block_mask.reshape(-1)

    q_shape = jax.ShapeDtypeStruct((groups, heads, tokens, HEAD_DIM), jnp.bfloat16)
    kv_send = pack_kv(key_rows, value_rows, (groups, 2, heads, tokens, HEAD_DIM))
    own = exchange(kv_send)
    q_send = call(pack_q_kernel, (after(query_rows, kv_send, place, mask),), q_shape)
    near = beside(after(out_weight, kv_send))

    first = to_frame(own, outward)
    second = to_frame(own, inward)
    queries = exchange(after(q_send, own))
    swapped = to_frame(after(own, queries), partner)
    half_shape = jax.ShapeDtypeStruct((near.shape[0], width // 2), jnp.bfloat16)
    near_half = call(half_kernel, (place, near), half_shape)
    mine = beside(near_half)
    far_first = to_frame(first, outward)
    far_second = to_frame(second, inward)
    swapped_first = to_frame(first, partner)
    far = to_frame(near, partner)
    other = to_frame(mine, partner)

    state = attend(((0, 0), (2, 1)), place, mask, queries, [own, swapped], None, False)
    slots, arrived = ((4, 3), (1, 2), (3, 4)), [first, swapped_first, second]
    state = attend(slots, place, mask, queries, arrived, state, False)
    state = attend(((6, 5),), place, mask, queries, [far_first], state, False)
    attention = attend(((5, 6),), place, mask, queries, [far_second], state, True)
    gathered = exchange(attention)
    return project(
        (place, levels), (gathered, near, far, other), (mine, out_weight, gate_table, residual)
    )


def solution(mesh):
    return jax.shard_map(
        body,
        mesh=mesh,
        in_specs=(
            P(("ctx", "head"), None),
            P(("ctx", "head"), None),
            P(("ctx", "head"), None),
            P(("ctx", "head"), None),
            P("ctx"),
            P(),
            P("ctx", None, None, None),
            P("head", None),
        ),
        out_specs=P(("ctx", "head"), None),
        check_vma=False,
    )
```

```python
import math

import jax
import jax.numpy as jnp
from jax import lax
from jax.experimental import pallas as pl
from jax.experimental.pallas import tpu as pltpu
from jax.sharding import PartitionSpec as P


HEAD_DIM = 128
BLOCK = 128
OWN = (0, 0)
EXP2_SCALE = math.log2(math.e) / math.sqrt(HEAD_DIM)
SMEM = pl.BlockSpec(memory_space=pltpu.SMEM)
VMEM = pl.BlockSpec(memory_space=pltpu.VMEM)


def to_frame(x, source_of):
    count = lax.axis_size("ctx")
    pairs = [(source_of(f), f) for f in range(count) if 0 <= source_of(f) < count]
    return lax.ppermute(x, "ctx", pairs)


def partner(f):
    return f ^ 1


def outward(f):
    return f + 2 if f % 2 == 0 else f - 2


def inward(f):
    return f - 2 if f % 2 == 0 else f + 2


def beside(x):
    frames, size = lax.axis_size("ctx"), lax.axis_size("head")
    pairs = [
        (f * size + (i + 1 - 2 * (f % 2)) % size, f * size + i)
        for f in range(frames)
        for i in range(size)
    ]
    return lax.ppermute(x, ("ctx", "head"), pairs)


def exchange(pieces):
    return lax.all_to_all(pieces, "head", 0, 0, tiled=True)


def call(kernel, args, out_shape, out_specs=None, scratch_shapes=()):
    specs = [SMEM if a.dtype == jnp.int32 else VMEM for a in args]
    args = [
        a if a.dtype == jnp.int32 else pltpu.with_memory_space_constraint(a, pltpu.VMEM)
        for a in args
    ]
    return pl.pallas_call(
        kernel,
        in_specs=specs,
        out_specs=out_specs or jax.tree.map(lambda _: VMEM, out_shape),
        scratch_shapes=scratch_shapes,
        out_shape=out_shape,
        compiler_params=pltpu.CompilerParams(vmem_limit_bytes=8 << 20),
    )(*args)


def pack_kv_kernel(key_hbm, value_hbm, out_hbm, value_ref, turned_ref, key_sems, sems):
    groups, _, heads = out_hbm.shape[:3]
    width = heads * HEAD_DIM
    fetches = [
        pltpu.make_async_copy(value_hbm.at[:, columns], value_ref.at[:, columns], sems.at[0, g])
        for g, columns in ((g, pl.ds(g * width, width)) for g in range(groups))
    ]
    keys = [
        pltpu.make_async_copy(
            key_hbm.at[:, pl.ds(i * HEAD_DIM, HEAD_DIM)],
            out_hbm.at[i // heads, 0, i % heads],
            key_sems.at[i],
        )
        for i in range(groups * heads)
    ]
    sends = [
        pltpu.make_async_copy(turned_ref.at[g], out_hbm.at[g, 1], sems.at[1, g])
        for g in range(groups)
    ]
    for copy in fetches + keys:
        copy.start()
    for g in range(groups):
        fetches[g].wait()
        for h in range(heads):
            at = slice((g * heads + h) * HEAD_DIM, (g * heads + h + 1) * HEAD_DIM)
            turned_ref[g, h] = jnp.transpose(value_ref[:, at])
        sends[g].start()
    for copy in keys + sends:
        copy.wait()


def pack_kv(key_rows, value_rows, shape):
    hbm = pl.BlockSpec(memory_space=pltpu.HBM)
    args = [pltpu.with_memory_space_constraint(a, pltpu.HBM) for a in (key_rows, value_rows)]
    return pl.pallas_call(
        pack_kv_kernel,
        in_specs=[hbm, hbm],
        out_specs=hbm,
        out_shape=jax.ShapeDtypeStruct(shape, jnp.bfloat16),
        scratch_shapes=[
            pltpu.VMEM(value_rows.shape, value_rows.dtype),
            pltpu.VMEM((shape[0], *shape[2:]), jnp.bfloat16),
            pltpu.SemaphoreType.DMA((shape[0] * shape[2],)),
            pltpu.SemaphoreType.DMA((2, shape[0])),
        ],
        name="pack_kv",
        compiler_params=pltpu.CompilerParams(vmem_limit_bytes=8 << 20),
    )(*args)


def pack_q_kernel(query_ref, out_ref):
    groups, heads = out_ref.shape[:2]
    for g in range(groups):
        for h in range(heads):
            out_ref[g, h] = query_ref[:, (g * heads + h) * HEAD_DIM : (g * heads + h + 1) * HEAD_DIM]


def half_kernel(place_ref, weight_ref, out_ref):
    width = out_ref.shape[1]
    out_ref[...] = weight_ref[:, pl.ds(pl.multiple_of(place_ref[0] * width, 128), width)]


def attend_kernel(slots, first, last, place_ref, mask_ref, q_ref, *refs):
    count = len(slots)
    kv_refs, refs = refs[:count], refs[count:]
    groups, heads = q_ref.shape[:2]
    rows = groups * BLOCK
    core = place_ref[0]
    if first:
        outs = refs
    else:
        peak_in, total_in, acc_in = refs[:3]
        outs = refs[3:]
    slot_at = [jnp.where(core == 0, even, odd) * groups * groups for even, odd in slots]
    keep = [
        [[mask_ref[slot_at[s] + a * groups + b] > 0 for a in range(groups)] for b in range(groups)]
        for s in range(count)
    ]
    ones = jnp.ones((16, count * rows), jnp.bfloat16)

    def score(h):
        keys = jnp.concatenate([kv[:, 0, h].reshape(rows, HEAD_DIM) for kv in kv_refs], axis=0)
        return lax.dot_general(
            keys,
            q_ref[:, h].reshape(rows, HEAD_DIM),
            (((1,), (1,)), ((), ())),
            preferred_element_type=jnp.float32,
        )

    def soften(h, scores):
        tiles, peak = [], None
        for i in range(count * groups):
            tile = scores[i * BLOCK : (i + 1) * BLOCK]
            if slots[i // groups] != OWN:
                tile = jnp.concatenate(
                    [
                        jnp.where(
                            keep[i // groups][i % groups][a],
                            tile[:, a * BLOCK : (a + 1) * BLOCK],
                            -jnp.inf,
                        )
                        for a in range(groups)
                    ],
                    axis=1,
                )
            top = jnp.max(tile.reshape(BLOCK // 8, 8, rows), axis=0)
            peak = top if peak is None else jnp.maximum(peak, top)
            tiles.append(tile)
        peak = jnp.max(peak, axis=0, keepdims=True)
        if not first:
            peak = jnp.maximum(peak, peak_in[h, 0:1])
        weights = [jnp.exp2((tile - peak) * EXP2_SCALE).astype(jnp.bfloat16) for tile in tiles]
        return peak, jnp.concatenate(weights, axis=0)

    def gather(h, peak, weights):
        values = jnp.concatenate(
            [kv[b, 1, h] for kv in kv_refs for b in range(groups)], axis=1
        )
        weighted = jnp.dot(
            jnp.concatenate([values, ones], axis=0), weights, preferred_element_type=jnp.float32
        )
        total, weighted = weighted[HEAD_DIM : HEAD_DIM + 8], weighted[:HEAD_DIM]
        if not first:
            rescale = jnp.exp2((peak_in[h, 0:1] - peak) * EXP2_SCALE)
            total = total + total_in[h] * rescale
            weighted = weighted + acc_in[h] * rescale
        if last:
            attention = (weighted / total[0:1]).astype(jnp.bfloat16)
            for a in range(groups):
                outs[1][a, h] = jnp.transpose(attention[:, a * BLOCK : (a + 1) * BLOCK])
            pltpu.make_async_copy(outs[1].at[:, h], outs[0].at[:, h], outs[2].at[h]).start()
        else:
            outs[0][h] = jnp.broadcast_to(peak, (8, rows))
            outs[1][h] = total
            outs[2][h] = weighted

    scores = score(0)
    for h in range(heads):
        ahead = score(h + 1) if h + 1 < heads else None
        gather(h, *soften(h, scores))
        scores = ahead
    if last:
        for h in range(heads):
            pltpu.make_async_copy(outs[1].at[:, h], outs[0].at[:, h], outs[2].at[h]).wait()


def attend(slots, place, mask, queries, kvs, state, last):
    groups, heads, tokens = queries.shape[:3]
    rows = groups * tokens
    out_specs, scratch_shapes = None, ()
    if last:
        out_shape = jax.ShapeDtypeStruct(queries.shape, jnp.bfloat16)
        out_specs = pl.BlockSpec(memory_space=pltpu.HBM)
        scratch_shapes = [
            pltpu.VMEM(queries.shape, jnp.bfloat16), pltpu.SemaphoreType.DMA((heads,))
        ]
    else:
        stat = jax.ShapeDtypeStruct((heads, 8, rows), jnp.float32)
        out_shape = [stat, stat, jax.ShapeDtypeStruct((heads, HEAD_DIM, rows), jnp.float32)]

    def kernel(*refs):
        attend_kernel(slots, state is None, last, *refs)

    args = (place, mask, queries, *kvs, *(state or ()))
    return call(kernel, args, out_shape, out_specs, scratch_shapes)


def project_kernel(
    place_ref, level_ref, o_ref, near_ref, far_ref, other_ref, mine_hbm, own_hbm, gate_hbm,
    residual_hbm, out_ref, mine_ref, own_ref, gate_ref, residual_ref, sems,
):
    pairs = (
        (mine_hbm, mine_ref), (own_hbm, own_ref), (gate_hbm, gate_ref),
        (residual_hbm, residual_ref),
    )
    copies = [pltpu.make_async_copy(*pair, sems.at[i]) for i, pair in enumerate(pairs)]
    for copy in copies:
        copy.start()
    groups, heads = o_ref.shape[:2]
    core, x = place_ref[0], place_ref[1]
    half = mine_ref.shape[1]

    def features(up):
        group = (x + up) % groups
        return jnp.concatenate([o_ref[group, h] for h in range(heads)], axis=1)

    step = 1 + 2 * core
    own, near, far, opposite = features(0), features(step), features(4 - step), features(2)
    ats = [pl.ds(pl.multiple_of(c * half, 128), half) for c in (core, 1 - core)]
    sums = [
        jnp.dot(near, near_ref[:, at], preferred_element_type=jnp.float32)
        + jnp.dot(far, far_ref[:, at], preferred_element_type=jnp.float32)
        for at in ats
    ]
    copies[0].wait()
    sums = [
        total + jnp.dot(opposite, opposite_ref[...], preferred_element_type=jnp.float32)
        for total, opposite_ref in zip(sums, (mine_ref, other_ref), strict=True)
    ]
    copies[1].wait()
    sums = [
        total + jnp.dot(own, own_ref[:, at], preferred_element_type=jnp.float32)
        for total, at in zip(sums, ats, strict=True)
    ]
    for copy in copies[2:]:
        copy.wait()
    for at, total in zip(ats, sums, strict=True):
        gate = gate_ref[pl.ds(level_ref[0], 1), at]
        mixed = residual_ref[:, at].astype(jnp.float32) + gate * total
        out_ref[:, at] = mixed.astype(jnp.bfloat16)


def project(scalars, resident, fetched):
    hbm = pl.BlockSpec(memory_space=pltpu.HBM)
    residual = fetched[-1]
    return pl.pallas_call(
        project_kernel,
        in_specs=[SMEM] * len(scalars) + [VMEM] * len(resident) + [hbm] * len(fetched),
        out_specs=VMEM,
        out_shape=jax.ShapeDtypeStruct(residual.shape, residual.dtype),
        scratch_shapes=[pltpu.VMEM(a.shape, a.dtype) for a in fetched]
        + [pltpu.SemaphoreType.DMA((len(fetched),))],
        name="project",
        compiler_params=pltpu.CompilerParams(vmem_limit_bytes=16 << 20),
    )(
        *scalars,
        *(pltpu.with_memory_space_constraint(a, pltpu.VMEM) for a in resident),
        *(pltpu.with_memory_space_constraint(a, pltpu.HBM) for a in fetched),
    )


def after(value, *others):
    return lax.optimization_barrier((value, *others))[0]


def body(query_rows, key_rows, value_rows, residual, levels, gate_table, block_mask, out_weight):
    groups = lax.axis_size("head")
    tokens, width = query_rows.shape
    heads = width // HEAD_DIM // groups
    core = lax.axis_index("ctx") % 2
    place = jnp.stack([core, lax.axis_index("head")])
    mask = block_mask.reshape(-1)

    q_shape = jax.ShapeDtypeStruct((groups, heads, tokens, HEAD_DIM), jnp.bfloat16)
    kv_send = pack_kv(key_rows, value_rows, (groups, 2, heads, tokens, HEAD_DIM))
    own = exchange(kv_send)
    q_send = call(pack_q_kernel, (after(query_rows, kv_send, place, mask),), q_shape)
    near = beside(after(out_weight, kv_send))

    first = to_frame(own, outward)
    second = to_frame(own, inward)
    queries = exchange(after(q_send, own))
    swapped = to_frame(after(own, queries), partner)
    half_shape = jax.ShapeDtypeStruct((near.shape[0], width // 2), jnp.bfloat16)
    near_half = call(half_kernel, (place, near), half_shape)
    mine = beside(near_half)
    far_first = to_frame(first, outward)
    far_second = to_frame(second, inward)
    swapped_first = to_frame(first, partner)
    far = to_frame(near, partner)
    other = to_frame(mine, partner)

    state = attend((OWN, (2, 1)), place, mask, queries, [own, swapped], None, False)
    slots, arrived = ((4, 3), (1, 2), (3, 4)), [first, swapped_first, second]
    state = attend(slots, place, mask, queries, arrived, state, False)
    state = attend(((6, 5),), place, mask, queries, [far_first], state, False)
    attention = attend(((5, 6),), place, mask, queries, [far_second], state, True)
    gathered = exchange(attention)
    return project(
        (place, levels), (gathered, near, far, other), (mine, out_weight, gate_table, residual)
    )


def solution(mesh):
    return jax.shard_map(
        body,
        mesh=mesh,
        in_specs=(
            P(("ctx", "head"), None),
            P(("ctx", "head"), None),
            P(("ctx", "head"), None),
            P(("ctx", "head"), None),
            P("ctx"),
            P(),
            P("ctx", None, None, None),
            P("head", None),
        ),
        out_specs=P(("ctx", "head"), None),
        check_vma=False,
    )
```

```python
import math

import jax
import jax.numpy as jnp
from jax import lax
from jax.experimental import pallas as pl
from jax.experimental.pallas import tpu as pltpu
from jax.sharding import PartitionSpec as P


HEAD_DIM = 128
BLOCK = 128
OWN = (0, 0)
EXP2_SCALE = math.log2(math.e) / math.sqrt(HEAD_DIM)
SMEM = pl.BlockSpec(memory_space=pltpu.SMEM)
VMEM = pl.BlockSpec(memory_space=pltpu.VMEM)


def to_frame(x, source_of):
    count = lax.axis_size("ctx")
    pairs = [(source_of(f), f) for f in range(count) if 0 <= source_of(f) < count]
    return lax.ppermute(x, "ctx", pairs)


def partner(f):
    return f ^ 1


def outward(f):
    return f + 2 if f % 2 == 0 else f - 2


def inward(f):
    return f - 2 if f % 2 == 0 else f + 2


def beside(x):
    frames, size = lax.axis_size("ctx"), lax.axis_size("head")
    pairs = [
        (f * size + (i + 1 - 2 * (f % 2)) % size, f * size + i)
        for f in range(frames)
        for i in range(size)
    ]
    return lax.ppermute(x, ("ctx", "head"), pairs)


def exchange(pieces):
    return lax.all_to_all(pieces, "head", 0, 0, tiled=True)


def call(kernel, args, out_shape, out_specs=None, scratch_shapes=()):
    specs = [SMEM if a.dtype == jnp.int32 else VMEM for a in args]
    args = [
        a if a.dtype == jnp.int32 else pltpu.with_memory_space_constraint(a, pltpu.VMEM)
        for a in args
    ]
    return pl.pallas_call(
        kernel,
        in_specs=specs,
        out_specs=out_specs or jax.tree.map(lambda _: VMEM, out_shape),
        scratch_shapes=scratch_shapes,
        out_shape=out_shape,
        compiler_params=pltpu.CompilerParams(vmem_limit_bytes=8 << 20),
    )(*args)


def pack_kv_kernel(key_hbm, value_hbm, out_hbm, key_ref, value_ref, out_ref, sems):
    groups, _, heads = out_ref.shape[:3]
    width = heads * HEAD_DIM
    fetches = [
        [
            pltpu.make_async_copy(hbm.at[:, columns], ref.at[:, columns], sems.at[i, g])
            for i, (hbm, ref) in enumerate(((key_hbm, key_ref), (value_hbm, value_ref)))
        ]
        for g, columns in ((g, pl.ds(g * width, width)) for g in range(groups))
    ]
    sends = [
        pltpu.make_async_copy(out_ref.at[g], out_hbm.at[g], sems.at[2, g]) for g in range(groups)
    ]
    for pair in fetches:
        for fetch in pair:
            fetch.start()
    for g in range(groups):
        for fetch in fetches[g]:
            fetch.wait()
        for h in range(heads):
            at = slice((g * heads + h) * HEAD_DIM, (g * heads + h + 1) * HEAD_DIM)
            out_ref[g, 0, h] = key_ref[:, at]
            out_ref[g, 1, h] = jnp.transpose(value_ref[:, at])
        sends[g].start()
    for send in sends:
        send.wait()


def pack_kv(key_rows, value_rows, shape):
    hbm = pl.BlockSpec(memory_space=pltpu.HBM)
    args = [pltpu.with_memory_space_constraint(a, pltpu.HBM) for a in (key_rows, value_rows)]
    return pl.pallas_call(
        pack_kv_kernel,
        in_specs=[hbm, hbm],
        out_specs=hbm,
        out_shape=jax.ShapeDtypeStruct(shape, jnp.bfloat16),
        scratch_shapes=[pltpu.VMEM(a.shape, a.dtype) for a in args]
        + [pltpu.VMEM(shape, jnp.bfloat16), pltpu.SemaphoreType.DMA((3, shape[0]))],
        name="pack_kv",
        compiler_params=pltpu.CompilerParams(vmem_limit_bytes=8 << 20),
    )(*args)


def pack_q_kernel(query_ref, out_ref):
    groups, heads = out_ref.shape[:2]
    for g in range(groups):
        for h in range(heads):
            out_ref[g, h] = query_ref[:, (g * heads + h) * HEAD_DIM : (g * heads + h + 1) * HEAD_DIM]


def half_kernel(place_ref, weight_ref, out_ref):
    width = out_ref.shape[1]
    out_ref[...] = weight_ref[:, pl.ds(pl.multiple_of(place_ref[0] * width, 128), width)]


def attend_kernel(slots, first, last, place_ref, mask_ref, q_ref, *refs):
    count = len(slots)
    kv_refs, refs = refs[:count], refs[count:]
    groups, heads = q_ref.shape[:2]
    rows = groups * BLOCK
    core = place_ref[0]
    if first:
        outs = refs
    else:
        peak_in, total_in, acc_in = refs[:3]
        outs = refs[3:]
    slot_at = [jnp.where(core == 0, even, odd) * groups * groups for even, odd in slots]
    keep = [
        [[mask_ref[slot_at[s] + a * groups + b] > 0 for a in range(groups)] for b in range(groups)]
        for s in range(count)
    ]
    ones = jnp.ones((16, count * rows), jnp.bfloat16)

    def score(h):
        keys = jnp.concatenate([kv[:, 0, h].reshape(rows, HEAD_DIM) for kv in kv_refs], axis=0)
        return lax.dot_general(
            keys,
            q_ref[:, h].reshape(rows, HEAD_DIM),
            (((1,), (1,)), ((), ())),
            preferred_element_type=jnp.float32,
        )

    def soften(h, scores):
        tiles, peak = [], None
        for i in range(count * groups):
            tile = scores[i * BLOCK : (i + 1) * BLOCK]
            if slots[i // groups] != OWN:
                tile = jnp.concatenate(
                    [
                        jnp.where(
                            keep[i // groups][i % groups][a],
                            tile[:, a * BLOCK : (a + 1) * BLOCK],
                            -jnp.inf,
                        )
                        for a in range(groups)
                    ],
                    axis=1,
                )
            top = jnp.max(tile.reshape(BLOCK // 8, 8, rows), axis=0)
            peak = top if peak is None else jnp.maximum(peak, top)
            tiles.append(tile)
        peak = jnp.max(peak, axis=0, keepdims=True)
        if not first:
            peak = jnp.maximum(peak, peak_in[h, 0:1])
        weights = [jnp.exp2((tile - peak) * EXP2_SCALE).astype(jnp.bfloat16) for tile in tiles]
        return peak, jnp.concatenate(weights, axis=0)

    def gather(h, peak, weights):
        values = jnp.concatenate(
            [kv[b, 1, h] for kv in kv_refs for b in range(groups)], axis=1
        )
        weighted = jnp.dot(
            jnp.concatenate([values, ones], axis=0), weights, preferred_element_type=jnp.float32
        )
        total, weighted = weighted[HEAD_DIM : HEAD_DIM + 8], weighted[:HEAD_DIM]
        if not first:
            rescale = jnp.exp2((peak_in[h, 0:1] - peak) * EXP2_SCALE)
            total = total + total_in[h] * rescale
            weighted = weighted + acc_in[h] * rescale
        if last:
            attention = (weighted / total[0:1]).astype(jnp.bfloat16)
            for a in range(groups):
                outs[1][a, h] = jnp.transpose(attention[:, a * BLOCK : (a + 1) * BLOCK])
            pltpu.make_async_copy(outs[1].at[:, h], outs[0].at[:, h], outs[2].at[h]).start()
        else:
            outs[0][h] = jnp.broadcast_to(peak, (8, rows))
            outs[1][h] = total
            outs[2][h] = weighted

    scores = score(0)
    for h in range(heads):
        ahead = score(h + 1) if h + 1 < heads else None
        gather(h, *soften(h, scores))
        scores = ahead
    if last:
        for h in range(heads):
            pltpu.make_async_copy(outs[1].at[:, h], outs[0].at[:, h], outs[2].at[h]).wait()


def attend(slots, place, mask, queries, kvs, state, last):
    groups, heads, tokens = queries.shape[:3]
    rows = groups * tokens
    out_specs, scratch_shapes = None, ()
    if last:
        out_shape = jax.ShapeDtypeStruct(queries.shape, jnp.bfloat16)
        out_specs = pl.BlockSpec(memory_space=pltpu.HBM)
        scratch_shapes = [
            pltpu.VMEM(queries.shape, jnp.bfloat16), pltpu.SemaphoreType.DMA((heads,))
        ]
    else:
        stat = jax.ShapeDtypeStruct((heads, 8, rows), jnp.float32)
        out_shape = [stat, stat, jax.ShapeDtypeStruct((heads, HEAD_DIM, rows), jnp.float32)]

    def kernel(*refs):
        attend_kernel(slots, state is None, last, *refs)

    args = (place, mask, queries, *kvs, *(state or ()))
    return call(kernel, args, out_shape, out_specs, scratch_shapes)


def project_kernel(
    place_ref, level_ref, o_ref, near_ref, far_ref, other_ref, mine_hbm, own_hbm, gate_hbm,
    residual_hbm, out_ref, mine_ref, own_ref, gate_ref, residual_ref, sems,
):
    pairs = (
        (mine_hbm, mine_ref), (own_hbm, own_ref), (gate_hbm, gate_ref),
        (residual_hbm, residual_ref),
    )
    copies = [pltpu.make_async_copy(*pair, sems.at[i]) for i, pair in enumerate(pairs)]
    for copy in copies:
        copy.start()
    groups, heads = o_ref.shape[:2]
    core, x = place_ref[0], place_ref[1]
    half = mine_ref.shape[1]

    def features(up):
        group = (x + up) % groups
        return jnp.concatenate([o_ref[group, h] for h in range(heads)], axis=1)

    step = 1 + 2 * core
    own, near, far, opposite = features(0), features(step), features(4 - step), features(2)
    ats = [pl.ds(pl.multiple_of(c * half, 128), half) for c in (core, 1 - core)]
    sums = [
        jnp.dot(near, near_ref[:, at], preferred_element_type=jnp.float32)
        + jnp.dot(far, far_ref[:, at], preferred_element_type=jnp.float32)
        for at in ats
    ]
    copies[0].wait()
    sums = [
        total + jnp.dot(opposite, opposite_ref[...], preferred_element_type=jnp.float32)
        for total, opposite_ref in zip(sums, (mine_ref, other_ref), strict=True)
    ]
    copies[1].wait()
    sums = [
        total + jnp.dot(own, own_ref[:, at], preferred_element_type=jnp.float32)
        for total, at in zip(sums, ats, strict=True)
    ]
    for copy in copies[2:]:
        copy.wait()
    for at, total in zip(ats, sums, strict=True):
        gate = gate_ref[pl.ds(level_ref[0], 1), at]
        mixed = residual_ref[:, at].astype(jnp.float32) + gate * total
        out_ref[:, at] = mixed.astype(jnp.bfloat16)


def project(scalars, resident, fetched):
    hbm = pl.BlockSpec(memory_space=pltpu.HBM)
    residual = fetched[-1]
    return pl.pallas_call(
        project_kernel,
        in_specs=[SMEM] * len(scalars) + [VMEM] * len(resident) + [hbm] * len(fetched),
        out_specs=VMEM,
        out_shape=jax.ShapeDtypeStruct(residual.shape, residual.dtype),
        scratch_shapes=[pltpu.VMEM(a.shape, a.dtype) for a in fetched]
        + [pltpu.SemaphoreType.DMA((len(fetched),))],
        name="project",
        compiler_params=pltpu.CompilerParams(vmem_limit_bytes=16 << 20),
    )(
        *scalars,
        *(pltpu.with_memory_space_constraint(a, pltpu.VMEM) for a in resident),
        *(pltpu.with_memory_space_constraint(a, pltpu.HBM) for a in fetched),
    )


def after(value, *others):
    return lax.optimization_barrier((value, *others))[0]


def body(query_rows, key_rows, value_rows, residual, levels, gate_table, block_mask, out_weight):
    groups = lax.axis_size("head")
    tokens, width = query_rows.shape
    heads = width // HEAD_DIM // groups
    core = lax.axis_index("ctx") % 2
    place = jnp.stack([core, lax.axis_index("head")])
    mask = block_mask.reshape(-1)

    q_shape = jax.ShapeDtypeStruct((groups, heads, tokens, HEAD_DIM), jnp.bfloat16)
    kv_send = pack_kv(key_rows, value_rows, (groups, 2, heads, tokens, HEAD_DIM))
    own = exchange(kv_send)
    q_send = call(pack_q_kernel, (after(query_rows, kv_send, place, mask),), q_shape)
    near = beside(after(out_weight, kv_send))

    first = to_frame(own, outward)
    second = to_frame(own, inward)
    queries = exchange(after(q_send, own))
    swapped = to_frame(after(own, queries), partner)
    half_shape = jax.ShapeDtypeStruct((near.shape[0], width // 2), jnp.bfloat16)
    near_half = call(half_kernel, (place, near), half_shape)
    mine = beside(near_half)
    far_first = to_frame(first, outward)
    far_second = to_frame(second, inward)
    swapped_first = to_frame(first, partner)
    far = to_frame(near, partner)
    other = to_frame(mine, partner)

    state = attend((OWN, (2, 1)), place, mask, queries, [own, swapped], None, False)
    slots, arrived = ((4, 3), (1, 2), (3, 4)), [first, swapped_first, second]
    state = attend(slots, place, mask, queries, arrived, state, False)
    state = attend(((6, 5),), place, mask, queries, [far_first], state, False)
    attention = attend(((5, 6),), place, mask, queries, [far_second], state, True)
    gathered = exchange(attention)
    return project(
        (place, levels), (gathered, near, far, other), (mine, out_weight, gate_table, residual)
    )


def solution(mesh):
    return jax.shard_map(
        body,
        mesh=mesh,
        in_specs=(
            P(("ctx", "head"), None),
            P(("ctx", "head"), None),
            P(("ctx", "head"), None),
            P(("ctx", "head"), None),
            P("ctx"),
            P(),
            P("ctx", None, None, None),
            P("head", None),
        ),
        out_specs=P(("ctx", "head"), None),
        check_vma=False,
    )
```
